32 devices in a mesh: db: 8 (over z, x), pb: 4 (over y, core).
Axes of the slice: x: 2, y: 2, z: 4, core: 2. Of those that a mesh axis runs over, the one named last changes fastest.
Arguments:
- queries: bfloat16 [256, 4096], P('pb'), may hold values from -6 to 6
- database: bfloat16 [8192, 4096], P(('db', 'pb')), may hold values from -6 to 6
- slopes: int32 [5], replicated, may hold values from 1 to 6, as said below
Outputs:
- match_score: float32 [256, 8192], P(None, ('db', 'pb'))
The draws below stay inside these ranges and needn't reach their ends.
Inputs may be any that keep to these rules, and one draw needn't show every extreme that they name: `slopes`: every slope lies in 1 to 6; one of them is 6 and one is 1.
All inputs are finite; a program needn't handle non-finite values.
Results may differ from the reference program's by a relative error of at most 0.0003.
Values may be sent and summed in bfloat16 or wider, within the bound.
A program may use at most 64 MiB of HBM per device.

```python
import jax
import jax.numpy as jnp
from jax import lax

D = 4096
DB_DEV = 256
SEQ = 20
RADIUS = 5
SLOPES = 5
SMAX = 6
NQ = 256
NDB = 8192


def draw_slopes(key, part):
    values = jax.random.randint(jax.random.fold_in(key, 11), (SLOPES,), 1, SMAX + 1)
    places = jax.random.permutation(jax.random.fold_in(key, 12), SLOPES)
    positions = jnp.arange(SLOPES)
    values = jnp.where(positions == places[0], SMAX, values)
    values = jnp.where(positions == places[1], 1, values)
    return values.astype(jnp.int32)


def block_levels(rng, dims, pieces, low, top_value):
    loudness = 1.0
    for position, parts in pieces:
        heights = jax.random.uniform(jax.random.fold_in(jax.random.fold_in(rng, 6), position), (parts,), jnp.float32, low / len(pieces), top_value / len(pieces))
        loudness = loudness * jnp.repeat(jnp.exp(heights), dims[position] // parts).reshape((-1,) + (1,) * (len(dims) - 1 - position))
    return loudness


def centred(key, extent, width, most, shards=(), kind=jnp.bfloat16):
    level = block_levels(key, extent, shards, -0.22, 0.18) if shards else 1.0
    entries = jax.random.normal(key, extent, jnp.float32) * width * level
    return jnp.minimum(jnp.maximum(entries, -most), most).astype(kind)


def setup_inputs(seed: int = 0) -> dict:
    splits = jax.random.split(jax.random.key(seed), 4)
    return {
        "queries": centred(splits[0], (NQ, D), 1.0, 6.0, ((0, 4),)),
        "database": centred(splits[1], (NDB, D), 1.0, 6.0, ((0, 32),)),
        "slopes": draw_slopes(jax.random.fold_in(splits[3], 71), 0),
    }


variance_floor = 0.25

def band_mask(first_frame, frame_count, band_total):
    frame_ids = first_frame + jnp.arange(frame_count, dtype=jnp.int32)
    inside = jnp.logical_and(frame_ids >= 0, frame_ids < band_total)
    return inside.astype(jnp.float32)[None, :]

def contrast(extended, validity):
    out_width = extended.shape[1] - 2 * RADIUS
    masked = extended * validity
    squared = masked * masked
    first_sum = masked[:, :out_width]
    second_sum = squared[:, :out_width]
    counted = validity[:, :out_width]
    for offset in range(1, 2 * RADIUS + 1):
        first_sum = first_sum + masked[:, offset:offset + out_width]
        second_sum = second_sum + squared[:, offset:offset + out_width]
        counted = counted + validity[:, offset:offset + out_width]
    counted = jnp.maximum(counted, 1.0)
    average = first_sum / counted
    spread = second_sum / counted - average * average
    center = extended[:, RADIUS:RADIUS + out_width]
    keeper = validity[:, RADIUS:RADIUS + out_width]
    return keeper * (center - average) / jnp.sqrt(jnp.maximum(spread, variance_floor))

def lagged(field, steps, slope):
    col_pad = steps * SMAX
    padded = jnp.pad(field, ((steps, 0), (col_pad, 0)))
    begin = (col_pad - steps * slope).astype(jnp.int32)
    return lax.dynamic_slice(padded, (jnp.int32(0), begin), field.shape)

def window_sum(field, slope):
    powers = [field]
    stride = 1
    while 2 * stride <= SEQ:
        powers.append(powers[-1] + lagged(powers[-1], stride, slope))
        stride = stride * 2
    summed = None
    filled = 0
    for level in reversed(range(len(powers))):
        if SEQ >> level & 1:
            segment = powers[level] if filled == 0 else lagged(powers[level], filled, slope)
            summed = segment if summed is None else summed + segment
            filled = filled + (1 << level)
    return summed

def best_match(joined, slopes, reach):
    highest = None
    for member in range(SLOPES):
        summed = window_sum(joined, slopes[member])[:, reach:]
        highest = summed if highest is None else jnp.maximum(highest, summed)
    return highest * SEQ ** (-0.5)

def reference(queries, database, slopes):
    band_total = database.shape[0]
    scale = database.shape[1] ** (-0.5)
    reach = SMAX * (SEQ - 1)
    padded = jnp.pad(database, ((reach + RADIUS, RADIUS), (0, 0)))
    blocks = band_total // DB_DEV
    starts = jnp.arange(blocks, dtype=jnp.int32) * DB_DEV
    span_len = DB_DEV + reach + 2 * RADIUS

    def one_block(start):
        rows_part = lax.dynamic_slice_in_dim(padded, start, span_len, 0)
        similar = jnp.dot(queries, rows_part.T, preferred_element_type=jnp.float32) * scale
        validity = band_mask(start - reach - RADIUS, span_len, band_total)
        joined = contrast(similar, validity)
        return best_match(joined, slopes, reach)
    results = lax.map(one_block, starts)
    return jnp.transpose(results, (1, 0, 2)).reshape(queries.shape[0], band_total)
```

```python
import functools

import jax
import jax.numpy as jnp
from jax import lax
from jax.experimental import pallas as pl
from jax.experimental.pallas import tpu as pltpu
from jax.sharding import PartitionSpec as P

SEQ = 20
RADIUS = 5
SLOPES = 5
SMAX = 6
CHUNKS = 4
LEFT = 128
RIGHT = 8
LANES = 128

variance_floor = 0.25
MESH = pl.DeviceIdType.MESH


def similarity_kernel(
    n_db, n_pb, q_ref, base_ref, out_ref, qbuf, base, left_in, right_in,
    load_sem, own_sem, far_send, far_recv, core_send, core_recv, fwd_send, fwd_recv, edge_send, edge_recv,
):
    db, pb = lax.axis_index("db"), lax.axis_index("pb")
    rows, depth = q_ref.shape
    frames = base_ref.shape[0]
    groups = n_pb // 2
    core, group = lax.rem(pb, 2), pb // 2
    mate = pb + 1 - 2 * core
    me = db * n_pb + pb
    total = n_db * n_pb
    far = [lax.rem(group + step, groups) * 2 + core for step in range(1, groups)]
    source = [lax.rem(group + groups - step, groups) * 2 + core for step in range(1, groups)]
    width = depth // CHUNKS
    has_left, has_right = me > 0, me < total - 1
    left, right = me - 1, me + 1

    load = pltpu.make_async_copy(base_ref, base, load_sem)
    load.start()
    own = pltpu.make_async_copy(q_ref, qbuf.at[pl.ds(pb * rows, rows), :], own_sem)
    own.start()

    barrier = pltpu.get_barrier_semaphore()
    for peer in [mate] + far:
        pl.semaphore_signal(barrier, inc=1, device_id={"db": db, "pb": peer}, device_id_type=MESH)

    @pl.when(has_left)
    def _():
        pl.semaphore_signal(barrier, inc=1, device_id={"db": left // n_pb, "pb": lax.rem(left, n_pb)}, device_id_type=MESH)

    @pl.when(has_right)
    def _():
        pl.semaphore_signal(barrier, inc=1, device_id={"db": right // n_pb, "pb": lax.rem(right, n_pb)}, device_id_type=MESH)

    pl.semaphore_wait(barrier, groups + has_left.astype(jnp.int32) + has_right.astype(jnp.int32))

    def piece(owner, chunk):
        return qbuf.at[pl.ds(owner * rows, rows), pl.ds(chunk * width, width)]

    sent = []
    for chunk in range(CHUNKS):
        for step, peer in enumerate(far):
            copy = pltpu.make_async_remote_copy(
                src_ref=q_ref.at[:, pl.ds(chunk * width, width)],
                dst_ref=piece(pb, chunk),
                send_sem=far_send.at[step, chunk],
                recv_sem=far_recv.at[step, chunk],
                device_id={"db": db, "pb": peer},
                device_id_type=MESH,
            )
            copy.start()
            sent.append(copy)
    near = pltpu.make_async_remote_copy(
        src_ref=q_ref,
        dst_ref=qbuf.at[pl.ds(pb * rows, rows), :],
        send_sem=core_send,
        recv_sem=core_recv,
        device_id={"db": db, "pb": mate},
        device_id_type=MESH,
    )
    near.start()
    load.wait()
    own.wait()
    near.wait()

    passed = [[] for _ in range(CHUNKS)]
    for chunk in range(CHUNKS):
        for step in range(groups - 1):
            pltpu.make_async_remote_copy(
                src_ref=piece(source[step], chunk),
                dst_ref=piece(source[step], chunk),
                send_sem=far_send.at[step, chunk],
                recv_sem=far_recv.at[step, chunk],
                device_id={"db": db, "pb": mate},
                device_id_type=MESH,
            ).wait_recv()
            copy = pltpu.make_async_remote_copy(
                src_ref=piece(source[step], chunk),
                dst_ref=piece(source[step], chunk),
                send_sem=fwd_send.at[step, chunk],
                recv_sem=fwd_recv.at[step, chunk],
                device_id={"db": db, "pb": mate},
                device_id_type=MESH,
            )
            copy.start()
            passed[chunk].append(copy)
        for copy in passed[chunk]:
            copy.wait_recv()
        cols = pl.ds(chunk * width, width)
        term = lax.dot_general(
            base[:, cols], qbuf[:, cols], (((1,), (1,)), ((), ())), preferred_element_type=jnp.float32
        )
        if chunk == 0:
            out_ref[pl.ds(LEFT, frames), :] = term
        elif chunk < CHUNKS - 1:
            out_ref[pl.ds(LEFT, frames), :] += term
        else:
            out_ref[pl.ds(LEFT, frames), :] = (out_ref[pl.ds(LEFT, frames), :] + term) * depth ** (-0.5)

    ahead = pltpu.make_async_remote_copy(
        src_ref=out_ref.at[pl.ds(frames, LEFT), :],
        dst_ref=left_in,
        send_sem=edge_send.at[0],
        recv_sem=edge_recv.at[0],
        device_id={"db": lax.rem(right // n_pb, n_db), "pb": lax.rem(right, n_pb)},
        device_id_type=MESH,
    )
    behind = pltpu.make_async_remote_copy(
        src_ref=out_ref.at[pl.ds(LEFT, RIGHT), :],
        dst_ref=right_in,
        send_sem=edge_send.at[1],
        recv_sem=edge_recv.at[1],
        device_id={"db": jnp.maximum(left, 0) // n_pb, "pb": lax.rem(jnp.maximum(left, 0), n_pb)},
        device_id_type=MESH,
    )

    @pl.when(has_right)
    def _():
        ahead.start()

    @pl.when(has_left)
    def _():
        behind.start()

    for copy in sent:
        copy.wait_send()
    for copies in passed:
        for copy in copies:
            copy.wait_send()

    @pl.when(has_left)
    def _():
        ahead.wait_recv()
        out_ref[pl.ds(0, LEFT), :] = left_in[...]
        behind.wait_send()

    @pl.when(me == 0)
    def _():
        out_ref[pl.ds(0, LEFT), :] = jnp.zeros((LEFT, out_ref.shape[1]), jnp.float32)

    @pl.when(has_right)
    def _():
        behind.wait_recv()
        out_ref[pl.ds(LEFT + frames, RIGHT), :] = right_in[...]
        ahead.wait_send()

    @pl.when(me == total - 1)
    def _():
        out_ref[pl.ds(LEFT + frames, RIGHT), :] = jnp.zeros((RIGHT, out_ref.shape[1]), jnp.float32)


def similarities(queries, database, n_db, n_pb):
    rows, depth = queries.shape
    frames = database.shape[0]
    nq = rows * n_pb
    groups = n_pb // 2
    far = (max(groups - 1, 1), CHUNKS)
    return pl.pallas_call(
        functools.partial(similarity_kernel, n_db, n_pb),
        out_shape=jax.ShapeDtypeStruct((LEFT + frames + RIGHT, nq), jnp.float32),
        in_specs=[pl.BlockSpec(memory_space=pl.ANY)] * 2,
        out_specs=pl.BlockSpec(memory_space=pltpu.VMEM),
        scratch_shapes=[
            pltpu.VMEM((nq, depth), jnp.bfloat16),
            pltpu.VMEM((frames, depth), jnp.bfloat16),
            pltpu.VMEM((LEFT, nq), jnp.float32),
            pltpu.VMEM((RIGHT, nq), jnp.float32),
            pltpu.SemaphoreType.DMA,
            pltpu.SemaphoreType.DMA,
            pltpu.SemaphoreType.DMA(far),
            pltpu.SemaphoreType.DMA(far),
            pltpu.SemaphoreType.DMA,
            pltpu.SemaphoreType.DMA,
            pltpu.SemaphoreType.DMA(far),
            pltpu.SemaphoreType.DMA(far),
            pltpu.SemaphoreType.DMA((2,)),
            pltpu.SemaphoreType.DMA((2,)),
        ],
        compiler_params=pltpu.CompilerParams(
            collective_id=0, has_side_effects=True, vmem_limit_bytes=48 * 1024 * 1024
        ),
    )(queries, database)


def score_kernel(band_total, n_pb, slopes_ref, sim_ref, out_ref, field, normed, two, four, eight, best):
    span, nq = sim_ref.shape
    frames = out_ref.shape[1]
    pieces = nq // LANES
    anchor = (lax.axis_index("db") * n_pb + lax.axis_index("pb")) * frames - LEFT

    ids = lax.broadcasted_iota(jnp.int32, (span, LANES), 0) + anchor
    inside = jnp.logical_and(ids >= 0, ids < band_total)
    for p in range(pieces):
        field[p] = jnp.where(inside, sim_ref[:, p * LANES : (p + 1) * LANES], 0.0)

    first, count = 8, span - 16
    center_ids = lax.broadcasted_iota(jnp.int32, (count, LANES), 0) + (anchor + first)
    counted = jnp.minimum(center_ids + RADIUS, band_total - 1) - jnp.maximum(center_ids - RADIUS, 0) + 1
    share = 1.0 / jnp.maximum(counted, 1).astype(jnp.float32)
    keep = jnp.logical_and(center_ids >= 0, center_ids < band_total)
    for p in range(pieces):
        first_sum = None
        for offset in range(-RADIUS, RADIUS + 1):
            part = field[p, pl.ds(first + offset, count), :]
            square = part * part
            first_sum = part if first_sum is None else first_sum + part
            second_sum = square if offset == -RADIUS else second_sum + square
        average = first_sum * share
        spread = second_sum * share - average * average
        center = field[p, pl.ds(first, count), :]
        value = (center - average) * lax.rsqrt(jnp.maximum(spread, variance_floor))
        normed[p, pl.ds(first, count), :] = jnp.where(keep, value, 0.0)

    def lagged(source, p, lo, steps, slope, lane):
        rows = span - RIGHT - lo
        begin = lo - steps * slope
        shifted = pltpu.roll(source[p, pl.ds(begin, rows), :], steps, 1)
        if p == 0:
            return jnp.where(lane[:rows] < steps, 0.0, shifted)
        earlier = pltpu.roll(source[p - 1, pl.ds(begin, rows), :], steps, 1)
        return jnp.where(lane[:rows] < steps, earlier, shifted)

    lane = lax.broadcasted_iota(jnp.int32, (span, LANES), 1)

    def member(index, carry):
        slope = slopes_ref[index]
        for source, target, lo, steps in (
            (normed, two, 16, 1),
            (two, four, 32, 2),
            (four, eight, 80, 4),
        ):
            for p in range(pieces):
                target[p, pl.ds(lo, span - RIGHT - lo), :] = source[p, pl.ds(lo, span - RIGHT - lo), :] + lagged(
                    source, p, lo, steps, slope, lane
                )
        for p in range(pieces):
            summed = eight[p, pl.ds(LEFT, frames), :] + lagged(eight, p, LEFT, 8, slope, lane)
            summed = summed + lagged(four, p, LEFT, 16, slope, lane)
            best[p] = jnp.maximum(best[p], summed)
        return carry

    best[...] = jnp.full(best.shape, -jnp.inf, jnp.float32)
    lax.fori_loop(0, slopes_ref.shape[0], member, 0)
    for p in range(pieces):
        out_ref[p * LANES : (p + 1) * LANES, :] = best[p].T * SEQ ** (-0.5)


def scores(similarity, slopes, band_total, n_pb):
    span, nq = similarity.shape
    frames = span - LEFT - RIGHT
    pieces = nq // LANES
    return pl.pallas_call(
        functools.partial(score_kernel, band_total, n_pb),
        out_shape=jax.ShapeDtypeStruct((nq, frames), jnp.float32),
        in_specs=[pl.BlockSpec(memory_space=pltpu.SMEM), pl.BlockSpec(memory_space=pltpu.VMEM)],
        out_specs=pl.BlockSpec(memory_space=pltpu.VMEM),
        scratch_shapes=[pltpu.VMEM((pieces, span, LANES), jnp.float32)] * 5
        + [pltpu.VMEM((pieces, frames, LANES), jnp.float32)],
        compiler_params=pltpu.CompilerParams(vmem_limit_bytes=48 * 1024 * 1024),
    )(slopes, similarity)


def on_device(n_db, n_pb, queries, database, slopes):
    similarity = similarities(queries, database, n_db, n_pb)
    return scores(similarity, slopes, database.shape[0] * n_db * n_pb, n_pb)


def solution(mesh):
    placed = (P("pb", None), P(("db", "pb"), None), P())
    sizes = (mesh.shape["db"], mesh.shape["pb"])
    return jax.shard_map(
        functools.partial(on_device, *sizes),
        mesh=mesh,
        in_specs=placed,
        out_specs=P(None, ("db", "pb")),
        check_vma=False,
    )
```

```python
import functools

import jax
import jax.numpy as jnp
from jax import lax
from jax.experimental import pallas as pl
from jax.experimental.pallas import tpu as pltpu
from jax.sharding import PartitionSpec as P

SEQ = 20
RADIUS = 5
SLOPES = 5
SMAX = 6
CHUNKS = 4
LEFT = 128
RIGHT = 8
LANES = 128

variance_floor = 0.25
MESH = pl.DeviceIdType.MESH


def similarity_kernel(
    n_db, n_pb, q_ref, base_ref, out_ref, qbuf, base, left_in, right_in,
    load_sem, own_sem, far_send, far_recv, core_send, core_recv, fwd_send, fwd_recv, edge_send, edge_recv,
):
    db, pb = lax.axis_index("db"), lax.axis_index("pb")
    rows, depth = q_ref.shape
    frames = base_ref.shape[0]
    groups = n_pb // 2
    core, group = lax.rem(pb, 2), pb // 2
    mate = pb + 1 - 2 * core
    me = db * n_pb + pb
    total = n_db * n_pb
    far = [lax.rem(group + step, groups) * 2 + core for step in range(1, groups)]
    source = [lax.rem(group + groups - step, groups) * 2 + core for step in range(1, groups)]
    width = depth // CHUNKS
    has_left, has_right = me > 0, me < total - 1
    left, right = me - 1, me + 1

    load = pltpu.make_async_copy(base_ref, base, load_sem)
    load.start()
    own = pltpu.make_async_copy(q_ref, qbuf.at[pl.ds(pb * rows, rows), :], own_sem)
    own.start()

    barrier = pltpu.get_barrier_semaphore()
    for peer in [mate] + far:
        pl.semaphore_signal(barrier, inc=1, device_id={"db": db, "pb": peer}, device_id_type=MESH)

    @pl.when(has_left)
    def _():
        pl.semaphore_signal(barrier, inc=1, device_id={"db": left // n_pb, "pb": lax.rem(left, n_pb)}, device_id_type=MESH)

    @pl.when(has_right)
    def _():
        pl.semaphore_signal(barrier, inc=1, device_id={"db": right // n_pb, "pb": lax.rem(right, n_pb)}, device_id_type=MESH)

    pl.semaphore_wait(barrier, groups + has_left.astype(jnp.int32) + has_right.astype(jnp.int32))

    def piece(owner, chunk):
        return qbuf.at[pl.ds(owner * rows, rows), pl.ds(chunk * width, width)]

    sent = []
    for chunk in range(CHUNKS):
        for step, peer in enumerate(far):
            copy = pltpu.make_async_remote_copy(
                src_ref=q_ref.at[:, pl.ds(chunk * width, width)],
                dst_ref=piece(pb, chunk),
                send_sem=far_send.at[step, chunk],
                recv_sem=far_recv.at[step, chunk],
                device_id={"db": db, "pb": peer},
                device_id_type=MESH,
            )
            copy.start()
            sent.append(copy)
    near = pltpu.make_async_remote_copy(
        src_ref=q_ref,
        dst_ref=qbuf.at[pl.ds(pb * rows, rows), :],
        send_sem=core_send,
        recv_sem=core_recv,
        device_id={"db": db, "pb": mate},
        device_id_type=MESH,
    )
    near.start()
    load.wait()
    own.wait()
    near.wait()

    passed = [[] for _ in range(CHUNKS)]
    for chunk in range(CHUNKS):
        for step in range(groups - 1):
            pltpu.make_async_remote_copy(
                src_ref=piece(source[step], chunk),
                dst_ref=piece(source[step], chunk),
                send_sem=far_send.at[step, chunk],
                recv_sem=far_recv.at[step, chunk],
                device_id={"db": db, "pb": mate},
                device_id_type=MESH,
            ).wait_recv()
            copy = pltpu.make_async_remote_copy(
                src_ref=piece(source[step], chunk),
                dst_ref=piece(source[step], chunk),
                send_sem=fwd_send.at[step, chunk],
                recv_sem=fwd_recv.at[step, chunk],
                device_id={"db": db, "pb": mate},
                device_id_type=MESH,
            )
            copy.start()
            passed[chunk].append(copy)
        for copy in passed[chunk]:
            copy.wait_recv()
        cols = pl.ds(chunk * width, width)
        term = lax.dot_general(
            base[:, cols], qbuf[:, cols], (((1,), (1,)), ((), ())), preferred_element_type=jnp.float32
        )
        if chunk == 0:
            out_ref[pl.ds(LEFT, frames), :] = term
        elif chunk < CHUNKS - 1:
            out_ref[pl.ds(LEFT, frames), :] += term
        else:
            out_ref[pl.ds(LEFT, frames), :] = (out_ref[pl.ds(LEFT, frames), :] + term) * depth ** (-0.5)

    ahead = pltpu.make_async_remote_copy(
        src_ref=out_ref.at[pl.ds(frames, LEFT), :],
        dst_ref=left_in,
        send_sem=edge_send.at[0],
        recv_sem=edge_recv.at[0],
        device_id={"db": lax.rem(right // n_pb, n_db), "pb": lax.rem(right, n_pb)},
        device_id_type=MESH,
    )
    behind = pltpu.make_async_remote_copy(
        src_ref=out_ref.at[pl.ds(LEFT, RIGHT), :],
        dst_ref=right_in,
        send_sem=edge_send.at[1],
        recv_sem=edge_recv.at[1],
        device_id={"db": jnp.maximum(left, 0) // n_pb, "pb": lax.rem(jnp.maximum(left, 0), n_pb)},
        device_id_type=MESH,
    )

    @pl.when(has_right)
    def _():
        ahead.start()

    @pl.when(has_left)
    def _():
        behind.start()

    for copy in sent:
        copy.wait_send()
    for copies in passed:
        for copy in copies:
            copy.wait_send()

    @pl.when(has_left)
    def _():
        ahead.wait_recv()
        out_ref[pl.ds(0, LEFT), :] = left_in[...]
        behind.wait_send()

    @pl.when(me == 0)
    def _():
        out_ref[pl.ds(0, LEFT), :] = jnp.zeros((LEFT, out_ref.shape[1]), jnp.float32)

    @pl.when(has_right)
    def _():
        behind.wait_recv()
        out_ref[pl.ds(LEFT + frames, RIGHT), :] = right_in[...]
        ahead.wait_send()

    @pl.when(me == total - 1)
    def _():
        out_ref[pl.ds(LEFT + frames, RIGHT), :] = jnp.zeros((RIGHT, out_ref.shape[1]), jnp.float32)


def similarities(queries, database, n_db, n_pb):
    rows, depth = queries.shape
    frames = database.shape[0]
    nq = rows * n_pb
    groups = n_pb // 2
    far = (max(groups - 1, 1), CHUNKS)
    return pl.pallas_call(
        functools.partial(similarity_kernel, n_db, n_pb),
        out_shape=jax.ShapeDtypeStruct((LEFT + frames + RIGHT, nq), jnp.float32),
        in_specs=[pl.BlockSpec(memory_space=pltpu.HBM)] * 2,
        out_specs=pl.BlockSpec(memory_space=pltpu.VMEM),
        scratch_shapes=[
            pltpu.VMEM((nq, depth), jnp.bfloat16),
            pltpu.VMEM((frames, depth), jnp.bfloat16),
            pltpu.VMEM((LEFT, nq), jnp.float32),
            pltpu.VMEM((RIGHT, nq), jnp.float32),
            pltpu.SemaphoreType.DMA,
            pltpu.SemaphoreType.DMA,
            pltpu.SemaphoreType.DMA(far),
            pltpu.SemaphoreType.DMA(far),
            pltpu.SemaphoreType.DMA,
            pltpu.SemaphoreType.DMA,
            pltpu.SemaphoreType.DMA(far),
            pltpu.SemaphoreType.DMA(far),
            pltpu.SemaphoreType.DMA((2,)),
            pltpu.SemaphoreType.DMA((2,)),
        ],
        compiler_params=pltpu.CompilerParams(
            collective_id=0, has_side_effects=True, vmem_limit_bytes=60 * 1024 * 1024
        ),
    )(queries, database)


def score_kernel(band_total, n_pb, slopes_ref, sim_ref, out_ref, field, normed, two, four, eight, best):
    span, nq = sim_ref.shape
    frames = out_ref.shape[1]
    pieces = nq // LANES
    anchor = (lax.axis_index("db") * n_pb + lax.axis_index("pb")) * frames - LEFT

    ids = lax.broadcasted_iota(jnp.int32, (span, LANES), 0) + anchor
    inside = jnp.logical_and(ids >= 0, ids < band_total)
    for p in range(pieces):
        field[p] = jnp.where(inside, sim_ref[:, p * LANES : (p + 1) * LANES], 0.0)

    first, count = 8, span - 16
    center_ids = lax.broadcasted_iota(jnp.int32, (count, LANES), 0) + (anchor + first)
    counted = jnp.minimum(center_ids + RADIUS, band_total - 1) - jnp.maximum(center_ids - RADIUS, 0) + 1
    share = 1.0 / jnp.maximum(counted, 1).astype(jnp.float32)
    keep = jnp.logical_and(center_ids >= 0, center_ids < band_total)
    for p in range(pieces):
        first_sum = None
        for offset in range(-RADIUS, RADIUS + 1):
            part = field[p, pl.ds(first + offset, count), :]
            square = part * part
            first_sum = part if first_sum is None else first_sum + part
            second_sum = square if offset == -RADIUS else second_sum + square
        average = first_sum * share
        spread = second_sum * share - average * average
        center = field[p, pl.ds(first, count), :]
        value = (center - average) * lax.rsqrt(jnp.maximum(spread, variance_floor))
        normed[p, pl.ds(first, count), :] = jnp.where(keep, value, 0.0)

    lane = lax.broadcasted_iota(jnp.int32, (1, LANES), 1)

    def lagged(source, lo, steps, slope):
        rows = span - RIGHT - lo
        earlier, parts = 0.0, []
        for p in range(pieces):
            rolled = pltpu.roll(source[p, pl.ds(lo - steps * slope, rows), :], steps, 1)
            parts.append(jnp.where(lane < steps, earlier, rolled))
            earlier = rolled
        return parts

    best[...] = jnp.full(best.shape, -jnp.inf, jnp.float32)
    for slope in range(1, SMAX + 1):
        present = slopes_ref[0] == slope
        for index in range(1, slopes_ref.shape[0]):
            present = jnp.logical_or(present, slopes_ref[index] == slope)

        @pl.when(present)
        def _():
            for source, target, lo, steps in ((normed, two, 16, 1), (two, four, 32, 2), (four, eight, 80, 4)):
                parts = lagged(source, lo, steps, slope)
                for p in range(pieces):
                    target[p, pl.ds(lo, span - RIGHT - lo), :] = source[p, pl.ds(lo, span - RIGHT - lo), :] + parts[p]
            upper = lagged(eight, LEFT, 8, slope)
            tail = lagged(four, LEFT, 16, slope)
            for p in range(pieces):
                summed = eight[p, pl.ds(LEFT, frames), :] + upper[p] + tail[p]
                best[p] = jnp.maximum(best[p], summed)

    for p in range(pieces):
        out_ref[p * LANES : (p + 1) * LANES, :] = best[p].T * SEQ ** (-0.5)


def scores(similarity, slopes, band_total, n_pb):
    span, nq = similarity.shape
    frames = span - LEFT - RIGHT
    pieces = nq // LANES
    return pl.pallas_call(
        functools.partial(score_kernel, band_total, n_pb),
        out_shape=jax.ShapeDtypeStruct((nq, frames), jnp.float32),
        in_specs=[pl.BlockSpec(memory_space=pltpu.SMEM), pl.BlockSpec(memory_space=pltpu.VMEM)],
        out_specs=pl.BlockSpec(memory_space=pltpu.VMEM),
        scratch_shapes=[pltpu.VMEM((pieces, span, LANES), jnp.float32)] * 5
        + [pltpu.VMEM((pieces, frames, LANES), jnp.float32)],
        compiler_params=pltpu.CompilerParams(vmem_limit_bytes=48 * 1024 * 1024),
    )(slopes, similarity)


def on_device(n_db, n_pb, queries, database, slopes):
    similarity = similarities(queries, database, n_db, n_pb)
    return scores(similarity, slopes, database.shape[0] * n_db * n_pb, n_pb)


def solution(mesh):
    placed = (P("pb", None), P(("db", "pb"), None), P())
    sizes = (mesh.shape["db"], mesh.shape["pb"])
    return jax.shard_map(
        functools.partial(on_device, *sizes),
        mesh=mesh,
        in_specs=placed,
        out_specs=P(None, ("db", "pb")),
        check_vma=False,
    )
```

```python
import functools

import jax
import jax.numpy as jnp
from jax import lax
from jax.experimental import pallas as pl
from jax.experimental.pallas import tpu as pltpu
from jax.sharding import PartitionSpec as P

SEQ = 20
RADIUS = 5
SLOPES = 5
SMAX = 6
CHUNKS = 4
LEFT = 128
RIGHT = 8

variance_floor = 0.25
MESH = pl.DeviceIdType.MESH


def similarity_kernel(
    n_db, n_pb, q_ref, base_ref, out_ref, qbuf, base, left_in, right_in,
    load_sem, own_sem, far_send, far_recv, core_send, core_recv, side_send, side_recv,
    fwd_send, fwd_recv, edge_send, edge_recv,
):
    db, pb = lax.axis_index("db"), lax.axis_index("pb")
    rows, depth = q_ref.shape
    frames = base_ref.shape[0]
    groups = n_pb // 2
    core, group = lax.rem(pb, 2), pb // 2
    mate = pb + 1 - 2 * core
    half = lax.rem(db, 2)
    buddy = db + 1 - 2 * half
    me = db * n_pb + pb
    total = n_db * n_pb
    far = [lax.rem(group + step, groups) * 2 + core for step in range(1, groups)]
    origin = [lax.rem(group + groups - step, groups) for step in range(1, groups)]
    width = depth // (2 * CHUNKS)
    has_left, has_right = me > 0, me < total - 1
    left, right = jnp.maximum(me - 1, 0), jnp.minimum(me + 1, total - 1)

    own = pltpu.make_async_copy(q_ref, qbuf.at[group, pl.ds(core * rows, rows), :], own_sem)
    own.start()
    load = pltpu.make_async_copy(base_ref, base, load_sem)
    load.start()

    def device(db, pb):
        return {"db": db, "pb": pb}

    barrier = pltpu.get_barrier_semaphore()
    for peer in [device(db, mate), device(buddy, pb)] + [device(db, peer) for peer in far]:
        pl.semaphore_signal(barrier, inc=1, device_id=peer, device_id_type=MESH)

    @pl.when(has_left)
    def _():
        pl.semaphore_signal(
            barrier, inc=1, device_id=device(left // n_pb, lax.rem(left, n_pb)), device_id_type=MESH
        )

    @pl.when(has_right)
    def _():
        pl.semaphore_signal(
            barrier, inc=1, device_id=device(right // n_pb, lax.rem(right, n_pb)), device_id_type=MESH
        )

    pl.semaphore_wait(barrier, groups + 1 + has_left.astype(jnp.int32) + has_right.astype(jnp.int32))

    def columns(part, chunk):
        return pl.ds(pl.multiple_of(part * (depth // 2) + chunk * width, width), width)

    def piece(block, side, part, chunk):
        return qbuf.at[block, pl.ds(side * rows, rows), columns(part, chunk)]

    def remote(src, dst, send, recv, target):
        return pltpu.make_async_remote_copy(
            src_ref=src, dst_ref=dst, send_sem=send, recv_sem=recv, device_id=target, device_id_type=MESH
        )

    sent = []

    def go(copy):
        copy.start()
        sent.append(copy)

    for chunk in range(CHUNKS):
        for step, peer in enumerate(far):
            go(
                remote(
                    q_ref.at[:, columns(half, chunk)],
                    piece(group, core, half, chunk),
                    far_send.at[step, chunk],
                    far_recv.at[step, chunk],
                    device(db, peer),
                )
            )
    near = remote(
        q_ref, qbuf.at[group, pl.ds(core * rows, rows), :], core_send, core_recv, device(db, mate)
    )
    go(near)
    load.wait()
    own.wait()

    def product(block, cols):
        return lax.dot_general(
            base[:, cols], qbuf[block, :, cols], (((1,), (1,)), ((), ())), preferred_element_type=jnp.float32
        )

    def ahead(block):
        return remote(
            out_ref.at[block, pl.ds(frames, LEFT), :],
            left_in.at[block],
            edge_send.at[0, block],
            edge_recv.at[0, block],
            device(right // n_pb, lax.rem(right, n_pb)),
        )

    def behind(block):
        return remote(
            out_ref.at[block, pl.ds(LEFT, RIGHT), :],
            right_in.at[block],
            edge_send.at[1, block],
            edge_recv.at[1, block],
            device(left // n_pb, lax.rem(left, n_pb)),
        )

    def send_edges(block):
        @pl.when(has_right)
        def _():
            ahead(block).start()

        @pl.when(has_left)
        def _():
            behind(block).start()

    scale = depth ** (-0.5)
    mine = pl.ds(LEFT, frames)

    def first(step, chunk):
        block = piece(origin[step], core, half, chunk)
        remote(block, block, far_send.at[step, chunk], far_recv.at[step, chunk], device(db, mate)).wait_recv()
        go(remote(block, block, side_send.at[step, chunk], side_recv.at[step, chunk], device(buddy, pb)))
        go(remote(block, block, fwd_send.at[0, step, chunk], fwd_recv.at[0, step, chunk], device(db, mate)))

    def second(step, chunk):
        block = piece(origin[step], core, 1 - half, chunk)
        remote(block, block, side_send.at[step, chunk], side_recv.at[step, chunk], device(db, mate)).wait_recv()
        go(remote(block, block, fwd_send.at[1, step, chunk], fwd_recv.at[1, step, chunk], device(db, mate)))

    def multiply(order, step, chunk):
        part = half if order == 0 else 1 - half
        block = piece(origin[step], 1 - core, part, chunk)
        remote(
            block, block, fwd_send.at[order, step, chunk], fwd_recv.at[order, step, chunk], device(db, mate)
        ).wait_recv()
        term = product(origin[step], columns(part, chunk))
        if order == 0 and chunk == 0:
            out_ref[origin[step], mine, :] = term
        elif order == 1 and chunk == CHUNKS - 1:
            out_ref[origin[step], mine, :] = (out_ref[origin[step], mine, :] + term) * scale
        else:
            out_ref[origin[step], mine, :] += term

    far_steps = range(groups - 1)
    for stage in range(CHUNKS + 2):
        for step in far_steps:
            if stage < CHUNKS:
                first(step, stage)
            if 1 <= stage <= CHUNKS:
                second(step, stage - 1)
        if stage == 0:
            near.wait_recv()
            out_ref[group, mine, :] = product(group, slice(None)) * scale
            send_edges(group)
        for step in far_steps:
            if 1 <= stage <= CHUNKS:
                multiply(0, step, stage - 1)
            if stage >= 2:
                multiply(1, step, stage - 2)
    for step in far_steps:
        send_edges(origin[step])

    for copy in sent:
        copy.wait_send()

    @pl.when(has_left)
    def _():
        for block in range(groups):
            ahead(block).wait_recv()
            out_ref[block, pl.ds(0, LEFT), :] = left_in[block]
            behind(block).wait_send()

    @pl.when(me == 0)
    def _():
        out_ref[:, pl.ds(0, LEFT), :] = jnp.zeros(left_in.shape, jnp.float32)

    @pl.when(has_right)
    def _():
        for block in range(groups):
            behind(block).wait_recv()
            out_ref[block, pl.ds(LEFT + frames, RIGHT), :] = right_in[block]
            ahead(block).wait_send()

    @pl.when(me == total - 1)
    def _():
        out_ref[:, pl.ds(LEFT + frames, RIGHT), :] = jnp.zeros(right_in.shape, jnp.float32)


def similarities(queries, database, n_db, n_pb):
    rows, depth = queries.shape
    frames = database.shape[0]
    groups = n_pb // 2
    far = (max(groups - 1, 1), CHUNKS)
    dma = pltpu.SemaphoreType.DMA
    return pl.pallas_call(
        functools.partial(similarity_kernel, n_db, n_pb),
        out_shape=jax.ShapeDtypeStruct((groups, LEFT + frames + RIGHT, 2 * rows), jnp.float32),
        in_specs=[pl.BlockSpec(memory_space=pltpu.HBM)] * 2,
        out_specs=pl.BlockSpec(memory_space=pltpu.VMEM),
        scratch_shapes=[
            pltpu.VMEM((groups, 2 * rows, depth), jnp.bfloat16),
            pltpu.VMEM((frames, depth), jnp.bfloat16),
            pltpu.VMEM((groups, LEFT, 2 * rows), jnp.float32),
            pltpu.VMEM((groups, RIGHT, 2 * rows), jnp.float32),
            dma, dma, dma(far), dma(far), dma, dma, dma(far), dma(far),
            dma((2, *far)), dma((2, *far)), dma((2, groups)), dma((2, groups)),
        ],
        compiler_params=pltpu.CompilerParams(
            collective_id=0, has_side_effects=True, vmem_limit_bytes=60 * 1024 * 1024
        ),
    )(queries, database)


def score_kernel(band_total, n_pb, slopes_ref, sim_ref, out_ref, field, normed, two, four, eight, best):
    pieces, span, width = sim_ref.shape
    frames = out_ref.shape[1]
    anchor = (lax.axis_index("db") * n_pb + lax.axis_index("pb")) * frames - LEFT

    ids = lax.broadcasted_iota(jnp.int32, (span, width), 0) + anchor
    inside = jnp.logical_and(ids >= 0, ids < band_total)
    for p in range(pieces):
        field[p] = jnp.where(inside, sim_ref[p], 0.0)

    first, count = 8, span - 16
    center_ids = lax.broadcasted_iota(jnp.int32, (count, width), 0) + (anchor + first)
    counted = jnp.minimum(center_ids + RADIUS, band_total - 1) - jnp.maximum(center_ids - RADIUS, 0) + 1
    share = 1.0 / jnp.maximum(counted, 1).astype(jnp.float32)
    keep = jnp.logical_and(center_ids >= 0, center_ids < band_total)
    for p in range(pieces):
        first_sum = None
        for offset in range(-RADIUS, RADIUS + 1):
            part = field[p, pl.ds(first + offset, count), :]
            square = part * part
            first_sum = part if first_sum is None else first_sum + part
            second_sum = square if offset == -RADIUS else second_sum + square
        average = first_sum * share
        spread = second_sum * share - average * average
        center = field[p, pl.ds(first, count), :]
        value = (center - average) * lax.rsqrt(jnp.maximum(spread, variance_floor))
        normed[p, pl.ds(first, count), :] = jnp.where(keep, value, 0.0)

    lane = lax.broadcasted_iota(jnp.int32, (1, width), 1)

    def lagged(source, lo, steps, slope):
        rows = span - RIGHT - lo
        earlier, parts = 0.0, []
        for p in range(pieces):
            rolled = pltpu.roll(source[p, pl.ds(lo - steps * slope, rows), :], steps, 1)
            parts.append(jnp.where(lane < steps, earlier, rolled))
            earlier = rolled
        return parts

    best[...] = jnp.full(best.shape, -jnp.inf, jnp.float32)
    for slope in range(1, SMAX + 1):
        present = slopes_ref[0] == slope
        for index in range(1, slopes_ref.shape[0]):
            present = jnp.logical_or(present, slopes_ref[index] == slope)

        @pl.when(present)
        def _():
            for source, target, lo, steps in ((normed, two, 16, 1), (two, four, 32, 2), (four, eight, 80, 4)):
                parts = lagged(source, lo, steps, slope)
                for p in range(pieces):
                    target[p, pl.ds(lo, span - RIGHT - lo), :] = source[p, pl.ds(lo, span - RIGHT - lo), :] + parts[p]
            upper = lagged(eight, LEFT, 8, slope)
            tail = lagged(four, LEFT, 16, slope)
            for p in range(pieces):
                summed = eight[p, pl.ds(LEFT, frames), :] + upper[p] + tail[p]
                best[p] = jnp.maximum(best[p], summed)

    for p in range(pieces):
        out_ref[p * width : (p + 1) * width, :] = best[p].T * SEQ ** (-0.5)


def scores(similarity, slopes, band_total, n_pb):
    pieces, span, width = similarity.shape
    frames = span - LEFT - RIGHT
    return pl.pallas_call(
        functools.partial(score_kernel, band_total, n_pb),
        out_shape=jax.ShapeDtypeStruct((pieces * width, frames), jnp.float32),
        in_specs=[pl.BlockSpec(memory_space=pltpu.SMEM), pl.BlockSpec(memory_space=pltpu.VMEM)],
        out_specs=pl.BlockSpec(memory_space=pltpu.VMEM),
        scratch_shapes=[pltpu.VMEM((pieces, span, width), jnp.float32)] * 5
        + [pltpu.VMEM((pieces, frames, width), jnp.float32)],
        compiler_params=pltpu.CompilerParams(vmem_limit_bytes=48 * 1024 * 1024),
    )(slopes, similarity)


def on_device(n_db, n_pb, queries, database, slopes):
    similarity = similarities(queries, database, n_db, n_pb)
    return scores(similarity, slopes, database.shape[0] * n_db * n_pb, n_pb)


def solution(mesh):
    placed = (P("pb", None), P(("db", "pb"), None), P())
    sizes = (mesh.shape["db"], mesh.shape["pb"])
    return jax.shard_map(
        functools.partial(on_device, *sizes),
        mesh=mesh,
        in_specs=placed,
        out_specs=P(None, ("db", "pb")),
        check_vma=False,
    )
```
